1024 devices in a mesh: space: 8 (over x_hi, core), modes: 128 (over z, x_lo, y).
Axes of the slice: x: 8 (x_hi: 4, x_lo: 2; x = x_hi * 2 + x_lo), y: 8, z: 8, core: 2. Of those that a mesh axis runs over, the one named last changes fastest.
Arguments:
- modes_field: float32 [24576, 256], P('space', 'modes'), may hold values from -6 to 6
- slopes: float32 [24576, 256], P('space', 'modes'), may hold values from -6 to 6
Outputs:
- tensor: float32 [256, 256, 256], P('space', 'modes')
The draws below stay inside these ranges and needn't reach their ends.
All inputs are finite; a program needn't handle non-finite values.
Results may differ from the reference program's by a relative error of at most 0.0001.
Values sent between devices are 32-bit elements; how exact they have to be, the bound alone decides.
No kernel may reach another device: no remote copies, remote signals or barrier semaphores. Data moves between devices by JAX's collectives and lax.ppermute only.
A program may use at most 32 MiB of HBM per device.

```python
import jax
import jax.numpy as jnp
from jax import lax

R = 256
ROWS = 24576


def block_scale(key, dims, pieces, least, largest):
    def one(dim, shards_of):
        steps = jax.random.uniform(jax.random.fold_in(jax.random.fold_in(key, 6), dim), (shards_of,), jnp.float32, least / len(pieces), largest / len(pieces))
        return jnp.repeat(jnp.exp(steps), dims[dim] // shards_of).reshape((-1,) + (1,) * (len(dims) - dim - 1))

    loudness = one(*pieces[0])
    for cut in pieces[1:]:
        loudness = loudness * one(*cut)
    return loudness


def centred(rng, dims, width, bound, pieces=(), kind=jnp.bfloat16):
    gain = block_scale(rng, dims, pieces, -0.22, 0.18) if pieces else 1.0
    entries = jax.random.normal(rng, dims, jnp.float32) * width * gain
    return jnp.minimum(jnp.maximum(entries, -bound), bound).astype(kind)


def setup_inputs(seed: int = 0) -> dict:
    streams_of = jax.random.split(jax.random.key(seed), 3)
    modes_field = centred(streams_of[0], (ROWS, R), 1.0, 6.0, ((0, 8), (1, 128)), jnp.float32)
    slopes = centred(streams_of[1], (ROWS, R), 1.0, 6.0, ((0, 8), (1, 128)), jnp.float32)
    return dict(modes_field=modes_field, slopes=slopes)


def reference(modes_field, slopes):
    factor = 1.0 / jnp.sqrt(jnp.float32(ROWS))

    def one_mode(column):
        weighted = column[:, None] * slopes * factor
        return jnp.dot(modes_field.T, weighted, precision=lax.Precision.HIGHEST, preferred_element_type=jnp.float32)
    slabs = lax.map(one_mode, modes_field.T)
    return jnp.transpose(slabs, (1, 0, 2))
```

```python
import functools
import math

import jax
import jax.numpy as jnp
from jax import lax
from jax.experimental import pallas as pl
from jax.experimental.pallas import tpu as pltpu
from jax.sharding import Mesh
from jax.sharding import PartitionSpec as P

AXES = ("xh", "core", "z", "xl", "yh", "yl")
SPACE = ("xh", "core")
MODES = ("z", "xl", "yh", "yl")
VMEM = pl.BlockSpec(memory_space=pltpu.VMEM)
SMEM = pl.BlockSpec(memory_space=pltpu.SMEM)


def spread_kernel(m_ref, s_ref, out_ref):
    rows = out_ref.shape[3]
    for half in range(2):
        cut = slice(half * rows, (half + 1) * rows)
        for y in range(8):
            out_ref[half, y, 0:2, :] = m_ref[:, cut]
            out_ref[half, y, 2:4, :] = s_ref[:, cut]


def pick_kernel(at_ref, near_ref, out_ref):
    yh, yl = at_ref[1], at_ref[2]
    for shard in range(5):
        y = 2 * shard + yl if shard < 4 else 2 * yh + 1 - yl
        for xl in range(2):
            piece = near_ref[xl, y, 0:2, :]
            for z in range(8):
                out_ref[z, shard, 2 * xl : 2 * xl + 2, :] = piece


def tensor_kernel(at_ref, near_ref, far_ref, keep_ref, send_ref, left, left2, mode_j, slope, prod_hi, prod_lo):
    core, yh, yl = at_ref[0], at_ref[1], at_ref[2]
    for rel in range(2):
        for xh in range(4):
            z = 2 * xh + (core if rel == 0 else 1 - core)
            for q in range(4):
                row = rel * 64 + xh * 16 + q * 4
                left[row : row + 4, :] = far_ref[z, q]
    whole = left[...]
    high = whole.astype(jnp.bfloat16)
    left2[0:128, :] = high
    left2[128:256, :] = (whole - high.astype(jnp.float32)).astype(jnp.bfloat16)
    for y in range(2):
        shard = jnp.where(yl == y, yh, 4)
        for z in range(8):
            for xl in range(2):
                row = z * 8 + xl * 4 + y * 2
                mode_j[row : row + 2, :] = far_ref[z, shard, 2 * xl : 2 * xl + 2, :]
    for xl in range(2):
        for y in range(8):
            row = xl * 16 + y * 2
            slope[row : row + 2, :] = near_ref[xl, y, 2:4, :]

    lane = lax.broadcasted_iota(jnp.int32, (8, 128), 1)
    nt = (((1,), (1,)), ((), ()))

    def group(g, carry):
        modes = mode_j[pl.ds(pl.multiple_of(g * 16, 16), 16), :]
        for j in range(16):
            prod = slope[...] * modes[j : j + 1, :]
            high = prod.astype(jnp.bfloat16)
            prod_hi[j * 32 : (j + 1) * 32, :] = high
            prod_lo[j * 32 : (j + 1) * 32, :] = (prod - high.astype(jnp.float32)).astype(jnp.bfloat16)
        one = lax.dot_general(prod_hi[...], left2[...], nt, preferred_element_type=jnp.float32)
        two = lax.dot_general(prod_lo[...], left2[0:128, :], nt, preferred_element_type=jnp.float32)
        both = one[:, 0:128] + (one[:, 128:256] + two)
        for t in range(4):
            tile = both[t * 128 : (t + 1) * 128, :].T
            z, xl = g * 2 + t // 2, t % 2
            for s in range(8):
                ref, xh = (keep_ref, s) if s < 4 else (send_ref, s - 4)
                top, low = tile[s * 16 : s * 16 + 8, :], tile[s * 16 + 8 : s * 16 + 16, :]
                ref[xh, z, xl, 0] = jnp.where(lane < 64, top, pltpu.roll(low, 64, 1))
                ref[xh, z, xl, 1] = jnp.where(lane < 64, pltpu.roll(top, 64, 1), low)
        return carry

    lax.fori_loop(0, 4, group, 0)


def finish_kernel(factor, parts_ref, out_ref):
    lane = lax.broadcasted_iota(jnp.int32, (8, 128), 1)
    for yl in range(2):
        sums = []
        for z in range(8):
            total = parts_ref[0, z, 0, yl]
            for xh in range(4):
                for xl in range(2):
                    if xh or xl:
                        total = total + parts_ref[xh, z, xl, yl]
            sums.append(total * factor)
        for h in range(2):
            for bj in range(2):
                for side in range(2):
                    wide = None
                    for p in range(4):
                        here = sums[side * 4 + p]
                        shift = (p * 32 - (h * 64 + bj * 32)) % 128
                        moved = pltpu.roll(here, shift, 1) if shift else here
                        wide = moved if wide is None else jnp.where(lane < p * 32, wide, moved)
                    for r in range(8):
                        q, xl, b = h * 2 + r // 4, (r // 2) % 2, r % 2
                        i = xl * 16 + (2 * q + yl) * 2 + b
                        out_ref[i, bj : bj + 1, side * 128 : (side + 1) * 128] = wide[r : r + 1, :]


def per_device(modes_field, slopes):
    rows = modes_field.shape[0]
    half = rows // 2
    f32 = jnp.float32
    shape = jax.ShapeDtypeStruct
    factor = 1.0 / math.sqrt(rows * lax.axis_size(SPACE))
    at = jnp.stack([lax.axis_index("core"), lax.axis_index("yh"), lax.axis_index("yl")]).astype(jnp.int32)
    spread = pl.pallas_call(
        spread_kernel, out_shape=shape((2, 8, 4, half), f32), in_specs=[VMEM, VMEM], out_specs=VMEM
    )(modes_field.T, slopes.T)
    near = lax.all_to_all(spread.reshape(16, 4, half), ("xl", "yh", "yl"), 0, 0, tiled=True)
    near = near.reshape(2, 8, 4, half)
    picked = pl.pallas_call(
        pick_kernel, out_shape=shape((8, 5, 4, half), f32), in_specs=[SMEM, VMEM], out_specs=VMEM
    )(at, near)
    far = lax.all_to_all(picked, "z", 0, 0, tiled=True)
    piece = shape((4, 8, 2, 2, 8, 128), f32)
    keep, send = pl.pallas_call(
        tensor_kernel,
        out_shape=(piece, piece),
        in_specs=[SMEM, VMEM, VMEM],
        out_specs=(VMEM, VMEM),
        scratch_shapes=[
            pltpu.VMEM((128, half), f32),
            pltpu.VMEM((256, half), jnp.bfloat16),
            pltpu.VMEM((64, half), f32),
            pltpu.VMEM((32, half), f32),
            pltpu.VMEM((512, half), jnp.bfloat16),
            pltpu.VMEM((512, half), jnp.bfloat16),
        ],
    )(at, near, far)
    pair = keep + lax.ppermute(send, "core", [(0, 1), (1, 0)])
    parts = lax.all_to_all(pair.reshape(128, 8, 128), ("xh", "z", "xl", "yl"), 0, 0, tiled=True)
    return pl.pallas_call(
        functools.partial(finish_kernel, factor), out_shape=shape((32, 2, 256), f32), in_specs=[VMEM], out_specs=VMEM
    )(parts.reshape(4, 8, 2, 2, 8, 128))


def solution(mesh):
    fine = Mesh(mesh.devices.reshape(4, 2, 8, 2, 4, 2), AXES)
    placed = P(SPACE, MODES)
    return jax.shard_map(
        per_device, mesh=fine, in_specs=(placed, placed), out_specs=P(SPACE, MODES, None), check_vma=False
    )
```

```python
import functools
import math

import jax
import jax.numpy as jnp
from jax import lax
from jax.experimental import pallas as pl
from jax.experimental.pallas import tpu as pltpu
from jax.sharding import Mesh
from jax.sharding import PartitionSpec as P

AXES = ("xh", "core", "z", "xl", "yh", "yl")
SPACE = ("xh", "core")
MODES = ("z", "xl", "yh", "yl")
VMEM = pl.BlockSpec(memory_space=pltpu.VMEM)
HBM = pl.BlockSpec(memory_space=pltpu.HBM)


def on_chip(x):
    return pltpu.with_memory_space_constraint(x, pltpu.VMEM)


def in_place(x):
    return pltpu.with_memory_space_constraint(x, pltpu.HBM)


def room(mib):
    return pltpu.CompilerParams(vmem_limit_bytes=mib << 20)


def spread_kernel(m_hbm, s_hbm, out_ref, m_ref, s_ref, sem):
    rows = out_ref.shape[3]
    copies = [pltpu.make_async_copy(m_hbm, m_ref, sem.at[0]), pltpu.make_async_copy(s_hbm, s_ref, sem.at[1])]
    for copy in copies:
        copy.start()
    for copy in copies:
        copy.wait()
    for half in range(2):
        cut = slice(half * rows, (half + 1) * rows)
        for y in range(8):
            out_ref[half, y, 0:2, :] = m_ref[:, cut]
            out_ref[half, y, 2:4, :] = s_ref[:, cut]


def pick_kernel(near_ref, out_ref):
    yh, yl = lax.axis_index("yh"), lax.axis_index("yl")
    for shard in range(5):
        y = 2 * shard + yl if shard < 4 else 2 * yh + 1 - yl
        for xl in range(2):
            piece = near_ref[xl, y, 0:2, :]
            out_ref[shard, 2 * xl : 2 * xl + 2, :] = piece


def tensor_kernel(near_ref, far_ref, keep_ref, send_ref, left, left2, mode_j, slope, prod_hi, prod_lo):
    core, yh, yl = lax.axis_index("core"), lax.axis_index("yh"), lax.axis_index("yl")
    for rel in range(2):
        for xh in range(4):
            z = 2 * xh + (core if rel == 0 else 1 - core)
            for q in range(4):
                row = rel * 64 + xh * 16 + q * 4
                left[row : row + 4, :] = far_ref[z, q]
    whole = left[...]
    high = whole.astype(jnp.bfloat16)
    left2[0:128, :] = high
    left2[128:256, :] = (whole - high.astype(jnp.float32)).astype(jnp.bfloat16)
    for y in range(2):
        shard = jnp.where(yl == y, yh, 4)
        for z in range(8):
            for xl in range(2):
                row = z * 8 + xl * 4 + y * 2
                mode_j[row : row + 2, :] = far_ref[z, shard, 2 * xl : 2 * xl + 2, :]
    for xl in range(2):
        for y in range(8):
            row = xl * 16 + y * 2
            slope[row : row + 2, :] = near_ref[xl, y, 2:4, :]

    lane = lax.broadcasted_iota(jnp.int32, (8, 128), 1)
    nt = (((1,), (1,)), ((), ()))

    def group(g, carry):
        modes = mode_j[pl.ds(pl.multiple_of(g * 16, 16), 16), :]
        for j in range(16):
            prod = slope[...] * modes[j : j + 1, :]
            high = prod.astype(jnp.bfloat16)
            prod_hi[j * 32 : (j + 1) * 32, :] = high
            prod_lo[j * 32 : (j + 1) * 32, :] = (prod - high.astype(jnp.float32)).astype(jnp.bfloat16)
        one = lax.dot_general(prod_hi[...], left2[...], nt, preferred_element_type=jnp.float32)
        two = lax.dot_general(prod_lo[...], left2[0:128, :], nt, preferred_element_type=jnp.float32)
        both = one[:, 0:128] + (one[:, 128:256] + two)
        for t in range(4):
            tile = both[t * 128 : (t + 1) * 128, :].T
            z, xl = g * 2 + t // 2, t % 2
            for s in range(8):
                ref, xh = (keep_ref, s) if s < 4 else (send_ref, s - 4)
                top, low = tile[s * 16 : s * 16 + 8, :], tile[s * 16 + 8 : s * 16 + 16, :]
                ref[xh, z, xl, 0] = jnp.where(lane < 64, top, pltpu.roll(low, 64, 1))
                ref[xh, z, xl, 1] = jnp.where(lane < 64, pltpu.roll(top, 64, 1), low)
        return carry

    lax.fori_loop(0, 4, group, 0)


def finish_kernel(factor, parts_ref, out_ref):
    lane = lax.broadcasted_iota(jnp.int32, (8, 128), 1)
    for yl in range(2):
        sums = []
        for z in range(8):
            total = parts_ref[0, z, 0, yl]
            for xh in range(4):
                for xl in range(2):
                    if xh or xl:
                        total = total + parts_ref[xh, z, xl, yl]
            sums.append(total * factor)
        for h in range(2):
            for bj in range(2):
                for side in range(2):
                    wide = None
                    for p in range(4):
                        here = sums[side * 4 + p]
                        shift = (p * 32 - (h * 64 + bj * 32)) % 128
                        moved = pltpu.roll(here, shift, 1) if shift else here
                        wide = moved if wide is None else jnp.where(lane < p * 32, wide, moved)
                    for r in range(8):
                        q, xl, b = h * 2 + r // 4, (r // 2) % 2, r % 2
                        i = xl * 16 + (2 * q + yl) * 2 + b
                        out_ref[i, bj : bj + 1, side * 128 : (side + 1) * 128] = wide[r : r + 1, :]


def per_device(modes_field, slopes):
    rows, own = modes_field.shape
    half = rows // 2
    f32 = jnp.float32
    factor = 1.0 / math.sqrt(rows * lax.axis_size(SPACE))
    spread = pl.pallas_call(
        spread_kernel,
        out_shape=pltpu.VMEM((2, 8, 4, half), f32),
        in_specs=[HBM, HBM],
        out_specs=VMEM,
        scratch_shapes=[
            pltpu.VMEM((own, rows), f32),
            pltpu.VMEM((own, rows), f32),
            pltpu.SemaphoreType.DMA((2,)),
        ],
        compiler_params=room(8),
    )(in_place(modes_field.T), in_place(slopes.T))
    near = lax.all_to_all(spread.reshape(16, 4, half), ("xl", "yh", "yl"), 0, 0, tiled=True)
    near = on_chip(near.reshape(2, 8, 4, half))
    picked = pl.pallas_call(
        pick_kernel,
        out_shape=pltpu.VMEM((5, 4, half), f32),
        in_specs=[VMEM],
        out_specs=VMEM,
        compiler_params=room(8),
    )(near)
    far = on_chip(lax.all_gather(picked, "z", axis=0))
    piece = pltpu.VMEM((4, 8, 2, 2, 8, 128), f32)
    keep, send = pl.pallas_call(
        tensor_kernel,
        out_shape=(piece, piece),
        in_specs=[VMEM, VMEM],
        out_specs=(VMEM, VMEM),
        scratch_shapes=[
            pltpu.VMEM((128, half), f32),
            pltpu.VMEM((256, half), jnp.bfloat16),
            pltpu.VMEM((64, half), f32),
            pltpu.VMEM((32, half), f32),
            pltpu.VMEM((512, half), jnp.bfloat16),
            pltpu.VMEM((512, half), jnp.bfloat16),
        ],
        compiler_params=room(24),
    )(near, far)
    pair = keep + lax.ppermute(send, "core", [(0, 1), (1, 0)])
    parts = lax.all_to_all(pair.reshape(128, 8, 128), ("xh", "z", "xl", "yl"), 0, 0, tiled=True)
    return pl.pallas_call(
        functools.partial(finish_kernel, factor),
        out_shape=jax.ShapeDtypeStruct((32, 2, 256), f32),
        in_specs=[VMEM],
        out_specs=VMEM,
        compiler_params=room(8),
    )(on_chip(parts.reshape(4, 8, 2, 2, 8, 128)))


def solution(mesh):
    fine = Mesh(mesh.devices.reshape(4, 2, 8, 2, 4, 2), AXES)
    placed = P(SPACE, MODES)
    return jax.shard_map(
        per_device, mesh=fine, in_specs=(placed, placed), out_specs=P(SPACE, MODES, None), check_vma=False
    )
```

```python
import functools
import math

import jax
import jax.numpy as jnp
from jax import lax
from jax.experimental import pallas as pl
from jax.experimental.pallas import tpu as pltpu
from jax.sharding import Mesh
from jax.sharding import PartitionSpec as P

AXES = ("xh", "core", "z", "xl", "yh", "yl")
SPACE = ("xh", "core")
MODES = ("z", "xl", "yh", "yl")
VMEM = pl.BlockSpec(memory_space=pltpu.VMEM)
HBM = pl.BlockSpec(memory_space=pltpu.HBM)


def on_chip(x):
    return pltpu.with_memory_space_constraint(x, pltpu.VMEM)


def in_place(x):
    return pltpu.with_memory_space_constraint(x, pltpu.HBM)


def room(mib):
    return pltpu.CompilerParams(vmem_limit_bytes=mib << 20)


def spread_kernel(m_hbm, s_hbm, out_ref, m_ref, s_ref, sem):
    rows = out_ref.shape[3]
    copies = [pltpu.make_async_copy(m_hbm, m_ref, sem.at[0]), pltpu.make_async_copy(s_hbm, s_ref, sem.at[1])]
    for copy in copies:
        copy.start()
    for copy in copies:
        copy.wait()
    for half in range(2):
        cut = slice(half * rows, (half + 1) * rows)
        for y in range(8):
            out_ref[half, y, 0:2, :] = m_ref[:, cut]
            out_ref[half, y, 2:4, :] = s_ref[:, cut]


def pick_kernel(near_ref, out_ref):
    yh, yl = lax.axis_index("yh"), lax.axis_index("yl")
    for shard in range(5):
        y = 2 * shard + yl if shard < 4 else 2 * yh + 1 - yl
        for xl in range(2):
            piece = near_ref[xl, y, 0:2, :]
            out_ref[shard, 2 * xl : 2 * xl + 2, :] = piece


def tensor_kernel(near_ref, far_ref, keep_ref, send_ref, left, left2, mode_j, slope, prod_hi, prod_lo):
    core, yh, yl = lax.axis_index("core"), lax.axis_index("yh"), lax.axis_index("yl")
    for rel in range(2):
        for xh in range(4):
            z = 2 * xh + (core if rel == 0 else 1 - core)
            for q in range(4):
                row = rel * 64 + xh * 16 + q * 4
                left[row : row + 4, :] = far_ref[z, q]
    whole = left[...]
    high = whole.astype(jnp.bfloat16)
    left2[0:128, :] = high
    left2[128:256, :] = (whole - high.astype(jnp.float32)).astype(jnp.bfloat16)
    for y in range(2):
        shard = jnp.where(yl == y, yh, 4)
        for z in range(8):
            for xl in range(2):
                row = z * 8 + xl * 4 + y * 2
                mode_j[row : row + 2, :] = far_ref[z, shard, 2 * xl : 2 * xl + 2, :]
    for xl in range(2):
        for y in range(8):
            row = xl * 16 + y * 2
            slope[row : row + 2, :] = near_ref[xl, y, 2:4, :]

    lane = lax.broadcasted_iota(jnp.int32, (8, 128), 1)
    nt = (((1,), (1,)), ((), ()))

    for g in range(2):
        high_ref, low_ref = prod_hi.at[g % 2], prod_lo.at[g % 2]
        modes = mode_j[g * 32 : (g + 1) * 32, :]
        for j in range(32):
            prod = slope[...] * modes[j : j + 1, :]
            high = prod.astype(jnp.bfloat16)
            high_ref[j * 32 : (j + 1) * 32, :] = high
            low_ref[j * 32 : (j + 1) * 32, :] = (prod - high.astype(jnp.float32)).astype(jnp.bfloat16)
        one = lax.dot_general(high_ref[...], left2[...], nt, preferred_element_type=jnp.float32)
        two = lax.dot_general(low_ref[...], left2[0:128, :], nt, preferred_element_type=jnp.float32)
        both = one[:, 0:128] + (one[:, 128:256] + two)
        for t in range(8):
            tile = both[t * 128 : (t + 1) * 128, :].T
            z, xl = g * 4 + t // 2, t % 2
            for s in range(8):
                ref, xh = (keep_ref, s) if s < 4 else (send_ref, s - 4)
                top, low = tile[s * 16 : s * 16 + 8, :], tile[s * 16 + 8 : s * 16 + 16, :]
                ref[xh, z, xl, 0] = jnp.where(lane < 64, top, pltpu.roll(low, 64, 1))
                ref[xh, z, xl, 1] = jnp.where(lane < 64, pltpu.roll(top, 64, 1), low)


def finish_kernel(factor, parts_ref, out_ref):
    lane = lax.broadcasted_iota(jnp.int32, (8, 128), 1)
    for yl in range(2):
        sums = []
        for z in range(8):
            total = parts_ref[0, z, 0, yl]
            for xh in range(4):
                for xl in range(2):
                    if xh or xl:
                        total = total + parts_ref[xh, z, xl, yl]
            sums.append(total * factor)
        for h in range(2):
            for bj in range(2):
                for side in range(2):
                    wide = None
                    for p in range(4):
                        here = sums[side * 4 + p]
                        shift = (p * 32 - (h * 64 + bj * 32)) % 128
                        moved = pltpu.roll(here, shift, 1) if shift else here
                        wide = moved if wide is None else jnp.where(lane < p * 32, wide, moved)
                    for r in range(8):
                        q, xl, b = h * 2 + r // 4, (r // 2) % 2, r % 2
                        i = xl * 16 + (2 * q + yl) * 2 + b
                        out_ref[i, bj : bj + 1, side * 128 : (side + 1) * 128] = wide[r : r + 1, :]


def per_device(modes_field, slopes):
    rows, own = modes_field.shape
    half = rows // 2
    f32 = jnp.float32
    factor = 1.0 / math.sqrt(rows * lax.axis_size(SPACE))
    spread = pl.pallas_call(
        spread_kernel,
        out_shape=pltpu.VMEM((2, 8, 4, half), f32),
        in_specs=[HBM, HBM],
        out_specs=VMEM,
        scratch_shapes=[
            pltpu.VMEM((own, rows), f32),
            pltpu.VMEM((own, rows), f32),
            pltpu.SemaphoreType.DMA((2,)),
        ],
        compiler_params=room(8),
    )(in_place(modes_field.T), in_place(slopes.T))
    near = lax.all_to_all(spread.reshape(16, 4, half), ("xl", "yh", "yl"), 0, 0, tiled=True)
    near = on_chip(near.reshape(2, 8, 4, half))
    picked = pl.pallas_call(
        pick_kernel,
        out_shape=pltpu.VMEM((5, 4, half), f32),
        in_specs=[VMEM],
        out_specs=VMEM,
        compiler_params=room(8),
    )(near)
    far = on_chip(lax.all_gather(picked, "z", axis=0))
    piece = pltpu.VMEM((4, 8, 2, 2, 8, 128), f32)
    keep, send = pl.pallas_call(
        tensor_kernel,
        out_shape=(piece, piece),
        in_specs=[VMEM, VMEM],
        out_specs=(VMEM, VMEM),
        scratch_shapes=[
            pltpu.VMEM((128, half), f32),
            pltpu.VMEM((256, half), jnp.bfloat16),
            pltpu.VMEM((64, half), f32),
            pltpu.VMEM((32, half), f32),
            pltpu.VMEM((2, 1024, half), jnp.bfloat16),
            pltpu.VMEM((2, 1024, half), jnp.bfloat16),
        ],
        compiler_params=room(24),
    )(near, far)
    pair = keep + lax.ppermute(send, "core", [(0, 1), (1, 0)])
    parts = lax.all_to_all(pair.reshape(128, 8, 128), ("xh", "z", "xl", "yl"), 0, 0, tiled=True)
    return pl.pallas_call(
        functools.partial(finish_kernel, factor),
        out_shape=jax.ShapeDtypeStruct((32, 2, 256), f32),
        in_specs=[VMEM],
        out_specs=VMEM,
        compiler_params=room(8),
    )(on_chip(parts.reshape(4, 8, 2, 2, 8, 128)))


def solution(mesh):
    fine = Mesh(mesh.devices.reshape(4, 2, 8, 2, 4, 2), AXES)
    placed = P(SPACE, MODES)
    return jax.shard_map(
        per_device, mesh=fine, in_specs=(placed, placed), out_specs=P(SPACE, MODES, None), check_vma=False
    )
```

```python
import functools
import math

import jax
import jax.numpy as jnp
from jax import lax
from jax.experimental import pallas as pl
from jax.experimental.pallas import tpu as pltpu
from jax.sharding import Mesh
from jax.sharding import PartitionSpec as P

AXES = ("xh", "core", "z", "xl", "yh", "yl")
SPACE = ("xh", "core")
MODES = ("z", "xl", "yh", "yl")
VMEM = pl.BlockSpec(memory_space=pltpu.VMEM)
HBM = pl.BlockSpec(memory_space=pltpu.HBM)


def on_chip(x):
    return pltpu.with_memory_space_constraint(x, pltpu.VMEM)


def in_place(x):
    return pltpu.with_memory_space_constraint(x, pltpu.HBM)


def room(mib):
    return pltpu.CompilerParams(vmem_limit_bytes=mib << 20)


def spread_kernel(m_hbm, s_hbm, out_ref, m_ref, s_ref, sem):
    rows = out_ref.shape[3]
    copies = [pltpu.make_async_copy(m_hbm, m_ref, sem.at[0]), pltpu.make_async_copy(s_hbm, s_ref, sem.at[1])]
    for copy in copies:
        copy.start()
    for copy in copies:
        copy.wait()
    for half in range(2):
        cut = slice(half * rows, (half + 1) * rows)
        for y in range(8):
            out_ref[half, y, 0:2, :] = m_ref[:, cut]
            out_ref[half, y, 2:4, :] = s_ref[:, cut]


def pick_kernel(near_ref, out_ref):
    yh, yl = lax.axis_index("yh"), lax.axis_index("yl")
    for shard in range(5):
        y = 2 * shard + yl if shard < 4 else 2 * yh + 1 - yl
        for xl in range(2):
            piece = near_ref[xl, y, 0:2, :]
            out_ref[shard, 2 * xl : 2 * xl + 2, :] = piece


def tensor_kernel(near_ref, far_ref, keep_ref, send_ref, left, left2, mode_j, slope, prod_hi, prod_lo):
    core, yh, yl = lax.axis_index("core"), lax.axis_index("yh"), lax.axis_index("yl")
    own_xl = lax.axis_index("xl")
    for rel in range(2):
        for xh in range(4):
            z = 2 * xh + (core if rel == 0 else 1 - core)
            for q in range(4):
                row = rel * 64 + xh * 16 + q * 4
                left[row : row + 4, :] = far_ref[z, q]
    whole = left[...]
    high = whole.astype(jnp.bfloat16)
    left2[0:128, :] = high
    left2[128:256, :] = (whole - high.astype(jnp.float32)).astype(jnp.bfloat16)
    for y in range(2):
        shard = jnp.where(yl == y, yh, 4)
        for z in range(8):
            for xl in range(2):
                row = z * 8 + xl * 4 + y * 2
                mode_j[row : row + 2, :] = far_ref[z, shard, 2 * xl : 2 * xl + 2, :]
    for xl in range(2):
        for y in range(8):
            row = xl * 16 + y * 2
            slope[row : row + 2, :] = near_ref[xl, y, 2:4, :]

    lane = lax.broadcasted_iota(jnp.int32, (8, 128), 1)
    nt = (((1,), (1,)), ((), ()))

    for g in range(2):
        high_ref, low_ref = prod_hi.at[g % 2], prod_lo.at[g % 2]
        modes = mode_j[g * 32 : (g + 1) * 32, :]
        for j in range(32):
            prod = slope[...] * modes[j : j + 1, :]
            high = prod.astype(jnp.bfloat16)
            high_ref[j * 32 : (j + 1) * 32, :] = high
            low_ref[j * 32 : (j + 1) * 32, :] = (prod - high.astype(jnp.float32)).astype(jnp.bfloat16)
        one = lax.dot_general(high_ref[...], left2[...], nt, preferred_element_type=jnp.float32)
        two = lax.dot_general(low_ref[...], left2[0:128, :], nt, preferred_element_type=jnp.float32)
        both = one[:, 0:128] + (one[:, 128:256] + two)
        for t in range(8):
            tile = both[t * 128 : (t + 1) * 128, :].T
            z, side = g * 4 + t // 2, jnp.where(own_xl == t % 2, 0, 1)
            for s in range(8):
                ref, xh = (keep_ref, s) if s < 4 else (send_ref, s - 4)
                top, low = tile[s * 16 : s * 16 + 8, :], tile[s * 16 + 8 : s * 16 + 16, :]
                ref[side, xh, z, 0] = jnp.where(lane < 64, top, pltpu.roll(low, 64, 1))
                ref[side, xh, z, 1] = jnp.where(lane < 64, pltpu.roll(top, 64, 1), low)


def join_kernel(keep_ref, here_ref, left_ref, right_ref, out_ref):
    for half, ref in ((0, left_ref), (1, right_ref)):
        cut = slice(2 * half, 2 * half + 2)
        out_ref[cut] = keep_ref[0, cut] + here_ref[0, cut] + ref[...]


def finish_kernel(factor, parts_ref, out_ref):
    lane = lax.broadcasted_iota(jnp.int32, (8, 128), 1)
    for yl in range(2):
        sums = []
        for z in range(8):
            total = parts_ref[0, z, yl]
            for xh in range(1, 4):
                total = total + parts_ref[xh, z, yl]
            sums.append(total * factor)
        for h in range(2):
            for bj in range(2):
                for side in range(2):
                    wide = None
                    for p in range(4):
                        here = sums[side * 4 + p]
                        shift = (p * 32 - (h * 64 + bj * 32)) % 128
                        moved = pltpu.roll(here, shift, 1) if shift else here
                        wide = moved if wide is None else jnp.where(lane < p * 32, wide, moved)
                    for r in range(8):
                        q, xl, b = h * 2 + r // 4, (r // 2) % 2, r % 2
                        i = xl * 16 + (2 * q + yl) * 2 + b
                        out_ref[i, bj : bj + 1, side * 128 : (side + 1) * 128] = wide[r : r + 1, :]


def per_device(modes_field, slopes):
    rows, own = modes_field.shape
    half = rows // 2
    f32 = jnp.float32
    factor = 1.0 / math.sqrt(rows * lax.axis_size(SPACE))
    spread = pl.pallas_call(
        spread_kernel,
        out_shape=pltpu.VMEM((2, 8, 4, half), f32),
        in_specs=[HBM, HBM],
        out_specs=VMEM,
        scratch_shapes=[
            pltpu.VMEM((own, rows), f32),
            pltpu.VMEM((own, rows), f32),
            pltpu.SemaphoreType.DMA((2,)),
        ],
        compiler_params=room(8),
    )(in_place(modes_field.T), in_place(slopes.T))
    near = lax.all_to_all(spread.reshape(16, 4, half), ("xl", "yh", "yl"), 0, 0, tiled=True)
    near = on_chip(near.reshape(2, 8, 4, half))
    picked = pl.pallas_call(
        pick_kernel,
        out_shape=pltpu.VMEM((5, 4, half), f32),
        in_specs=[VMEM],
        out_specs=VMEM,
        compiler_params=room(8),
    )(near)
    far = on_chip(lax.all_gather(picked, "z", axis=0))
    piece = pltpu.VMEM((2, 4, 8, 2, 8, 128), f32)
    keep, send = pl.pallas_call(
        tensor_kernel,
        out_shape=(piece, piece),
        in_specs=[VMEM, VMEM],
        out_specs=(VMEM, VMEM),
        scratch_shapes=[
            pltpu.VMEM((128, half), f32),
            pltpu.VMEM((256, half), jnp.bfloat16),
            pltpu.VMEM((64, half), f32),
            pltpu.VMEM((32, half), f32),
            pltpu.VMEM((2, 1024, half), jnp.bfloat16),
            pltpu.VMEM((2, 1024, half), jnp.bfloat16),
        ],
        compiler_params=room(24),
    )(near, far)
    here = lax.ppermute(send, "core", [(0, 1), (1, 0)])
    chips = 2 * lax.axis_size("xh")
    left = lax.ppermute(keep[1, :2] + here[1, :2], ("xh", "xl"), [(x, (x + 1) % chips) for x in range(chips)])
    right = lax.ppermute(keep[1, 2:] + here[1, 2:], ("xh", "xl"), [((x + 1) % chips, x) for x in range(chips)])
    pair = pl.pallas_call(
        join_kernel,
        out_shape=pltpu.VMEM((4, 8, 2, 8, 128), f32),
        in_specs=[VMEM] * 4,
        out_specs=VMEM,
        compiler_params=room(8),
    )(*map(on_chip, (keep, here, left, right)))
    parts = lax.all_to_all(pair.reshape(64, 8, 128), ("xh", "z", "yl"), 0, 0, tiled=True)
    return pl.pallas_call(
        functools.partial(finish_kernel, factor),
        out_shape=jax.ShapeDtypeStruct((32, 2, 256), f32),
        in_specs=[VMEM],
        out_specs=VMEM,
        compiler_params=room(8),
    )(on_chip(parts.reshape(4, 8, 2, 8, 128)))


def solution(mesh):
    fine = Mesh(mesh.devices.reshape(4, 2, 8, 2, 4, 2), AXES)
    placed = P(SPACE, MODES)
    return jax.shard_map(
        per_device, mesh=fine, in_specs=(placed, placed), out_specs=P(SPACE, MODES, None), check_vma=False
    )
```

```python
import functools
import math

import jax
import jax.numpy as jnp
from jax import lax
from jax.experimental import pallas as pl
from jax.experimental.pallas import tpu as pltpu
from jax.sharding import Mesh
from jax.sharding import PartitionSpec as P

AXES = ("xh", "core", "z", "xl", "yh", "yl")
SPACE = ("xh", "core")
MODES = ("z", "xl", "yh", "yl")
VMEM = pl.BlockSpec(memory_space=pltpu.VMEM)
HBM = pl.BlockSpec(memory_space=pltpu.HBM)


def on_chip(x):
    return pltpu.with_memory_space_constraint(x, pltpu.VMEM)


def in_place(x):
    return pltpu.with_memory_space_constraint(x, pltpu.HBM)


def room(mib):
    return pltpu.CompilerParams(vmem_limit_bytes=mib << 20)


def spread_kernel(m_hbm, s_hbm, out_ref, m_ref, s_ref, sem):
    rows = out_ref.shape[3]
    copies = [pltpu.make_async_copy(m_hbm, m_ref, sem.at[0]), pltpu.make_async_copy(s_hbm, s_ref, sem.at[1])]
    for copy in copies:
        copy.start()
    for copy in copies:
        copy.wait()
    for half in range(2):
        cut = slice(half * rows, (half + 1) * rows)
        for y in range(8):
            out_ref[half, y, 0:2, :] = m_ref[:, cut]
            out_ref[half, y, 2:4, :] = s_ref[:, cut]


def pick_kernel(near_ref, out_ref):
    core, yh, yl = lax.axis_index("core"), lax.axis_index("yh"), lax.axis_index("yl")
    z = lax.axis_index("z")

    def put(piece, p, column):
        for xl in range(2):
            data = near_ref[xl, p, column : column + 2, :]
            for peer in range(8):
                out_ref[peer, piece, 2 * xl : 2 * xl + 2, :] = data

    for piece in range(8):
        y = 2 * piece + yl if piece < 4 else 2 * yh + 1 - yl
        put(piece, jnp.where(core == 0, y, piece), 0)
    put(8, z, 2)


def tensor_kernel(near_ref, far_ref, keep_ref, send_ref, left, left2, mode_j, slope, prod_hi, prod_lo):
    core, yh, yl = lax.axis_index("core"), lax.axis_index("yh"), lax.axis_index("yl")

    def far(z, y, piece):
        return jnp.where(core == 0, z, y), jnp.where(core == 0, piece, z)

    for rel in range(2):
        for xh in range(4):
            z = 2 * xh + (core if rel == 0 else 1 - core)
            for q in range(4):
                row = rel * 64 + xh * 16 + q * 4
                peer, piece = far(z, 2 * q + yl, q)
                left[row : row + 4, :] = far_ref[peer, piece]
    for y in range(2):
        for z in range(8):
            peer, piece = far(z, 2 * yh + y, jnp.where(yl == y, yh, 4))
            for xl in range(2):
                row = z * 8 + xl * 4 + y * 2
                mode_j[row : row + 2, :] = far_ref[peer, piece, 2 * xl : 2 * xl + 2, :]

    @pl.when(core == 0)
    def _():
        for xl in range(2):
            for y in range(8):
                row = xl * 16 + y * 2
                slope[row : row + 2, :] = near_ref[xl, y, 2:4, :]

    @pl.when(core != 0)
    def _():
        for xl in range(2):
            for y in range(8):
                row = xl * 16 + y * 2
                slope[row : row + 2, :] = far_ref[y, 8, 2 * xl : 2 * xl + 2, :]

    whole = left[...]
    high = whole.astype(jnp.bfloat16)
    left2[0:128, :] = high
    left2[128:256, :] = (whole - high.astype(jnp.float32)).astype(jnp.bfloat16)
    lane = lax.broadcasted_iota(jnp.int32, (8, 128), 1)
    nt = (((1,), (1,)), ((), ()))

    for g in range(2):
        high_ref, low_ref = prod_hi.at[g % 2], prod_lo.at[g % 2]
        modes = mode_j[g * 32 : (g + 1) * 32, :]
        for j in range(32):
            prod = slope[...] * modes[j : j + 1, :]
            high = prod.astype(jnp.bfloat16)
            high_ref[j * 32 : (j + 1) * 32, :] = high
            low_ref[j * 32 : (j + 1) * 32, :] = (prod - high.astype(jnp.float32)).astype(jnp.bfloat16)
        one = lax.dot_general(high_ref[...], left2[...], nt, preferred_element_type=jnp.float32)
        two = lax.dot_general(low_ref[...], left2[0:128, :], nt, preferred_element_type=jnp.float32)
        both = one[:, 0:128] + (one[:, 128:256] + two)
        for t in range(8):
            tile = both[t * 128 : (t + 1) * 128, :].T
            z, xl = g * 4 + t // 2, t % 2
            for s in range(8):
                ref, xh = (keep_ref, s) if s < 4 else (send_ref, s - 4)
                top, low = tile[s * 16 : s * 16 + 8, :], tile[s * 16 + 8 : s * 16 + 16, :]
                ref[xh, z, xl, 0] = jnp.where(lane < 64, top, pltpu.roll(low, 64, 1))
                ref[xh, z, xl, 1] = jnp.where(lane < 64, pltpu.roll(top, 64, 1), low)


def finish_kernel(factor, parts_ref, out_ref):
    lane = lax.broadcasted_iota(jnp.int32, (8, 128), 1)
    for yl in range(2):
        sums = []
        for z in range(8):
            total = parts_ref[0, z, 0, yl]
            for xh in range(4):
                for xl in range(2):
                    if xh or xl:
                        total = total + parts_ref[xh, z, xl, yl]
            sums.append(total * factor)
        for h in range(2):
            for bj in range(2):
                for side in range(2):
                    wide = None
                    for p in range(4):
                        here = sums[side * 4 + p]
                        shift = (p * 32 - (h * 64 + bj * 32)) % 128
                        moved = pltpu.roll(here, shift, 1) if shift else here
                        wide = moved if wide is None else jnp.where(lane < p * 32, wide, moved)
                    for r in range(8):
                        q, xl, b = h * 2 + r // 4, (r // 2) % 2, r % 2
                        i = xl * 16 + (2 * q + yl) * 2 + b
                        out_ref[i, bj : bj + 1, side * 128 : (side + 1) * 128] = wide[r : r + 1, :]


def gather_groups():
    first, second = [], []
    for xh in range(4):
        for core in range(2):
            for kept in range(8):
                for xl in range(2):
                    line = []
                    for moved in range(8):
                        z, y = (kept, moved) if core == 0 else (moved, kept)
                        line.append((((xh * 2 + core) * 8 + z) * 2 + xl) * 8 + y)
                    first.append(line)
    first = [first[n] + first[n + 1] for n in range(0, len(first), 2)]
    for xh in range(4):
        for core in range(2):
            for xl in range(2):
                for kept in range(8):
                    line = []
                    for moved in range(8):
                        z, y = (moved, kept) if core == 0 else (kept, moved)
                        line.append((((xh * 2 + core) * 8 + z) * 2 + xl) * 8 + y)
                    second.append(line)
    return first, second


def per_device(modes_field, slopes):
    rows, own = modes_field.shape
    half = rows // 2
    f32 = jnp.float32
    factor = 1.0 / math.sqrt(rows * lax.axis_size(SPACE))
    spread = pl.pallas_call(
        spread_kernel,
        out_shape=pltpu.VMEM((2, 8, 4, half), f32),
        in_specs=[HBM, HBM],
        out_specs=VMEM,
        scratch_shapes=[
            pltpu.VMEM((own, rows), f32),
            pltpu.VMEM((own, rows), f32),
            pltpu.SemaphoreType.DMA((2,)),
        ],
        compiler_params=room(8),
    )(in_place(modes_field.T), in_place(slopes.T))
    first, second = gather_groups()
    near = lax.all_to_all(spread.reshape(16, 4, half), AXES, 0, 0, axis_index_groups=first, tiled=True)
    near = on_chip(near.reshape(2, 8, 4, half))
    picked = pl.pallas_call(
        pick_kernel,
        out_shape=pltpu.VMEM((8, 9, 4, half), f32),
        in_specs=[VMEM],
        out_specs=VMEM,
        compiler_params=room(8),
    )(near)
    far = on_chip(lax.all_to_all(picked, AXES, 0, 0, axis_index_groups=second, tiled=True))
    piece = pltpu.VMEM((4, 8, 2, 2, 8, 128), f32)
    keep, send = pl.pallas_call(
        tensor_kernel,
        out_shape=(piece, piece),
        in_specs=[VMEM, VMEM],
        out_specs=(VMEM, VMEM),
        scratch_shapes=[
            pltpu.VMEM((128, half), f32),
            pltpu.VMEM((256, half), jnp.bfloat16),
            pltpu.VMEM((64, half), f32),
            pltpu.VMEM((32, half), f32),
            pltpu.VMEM((2, 1024, half), jnp.bfloat16),
            pltpu.VMEM((2, 1024, half), jnp.bfloat16),
        ],
        compiler_params=room(24),
    )(near, far)
    pair = keep + lax.ppermute(send, "core", [(0, 1), (1, 0)])
    parts = lax.all_to_all(pair.reshape(128, 8, 128), ("xh", "z", "xl", "yl"), 0, 0, tiled=True)
    return pl.pallas_call(
        functools.partial(finish_kernel, factor),
        out_shape=jax.ShapeDtypeStruct((32, 2, 256), f32),
        in_specs=[VMEM],
        out_specs=VMEM,
        compiler_params=room(8),
    )(on_chip(parts.reshape(4, 8, 2, 2, 8, 128)))


def solution(mesh):
    fine = Mesh(mesh.devices.reshape(4, 2, 8, 2, 4, 2), AXES)
    placed = P(SPACE, MODES)
    return jax.shard_map(
        per_device, mesh=fine, in_specs=(placed, placed), out_specs=P(SPACE, MODES, None), check_vma=False
    )
```

```python
import functools
import math

import jax
import jax.numpy as jnp
from jax import lax
from jax.experimental import pallas as pl
from jax.experimental.pallas import tpu as pltpu
from jax.sharding import Mesh
from jax.sharding import PartitionSpec as P

AXES = ("xh", "core", "zh", "zl", "xl", "yh", "yl")
SPACE = ("xh", "core")
MODES = ("zh", "zl", "xl", "yh", "yl")
VMEM = pl.BlockSpec(memory_space=pltpu.VMEM)
HBM = pl.BlockSpec(memory_space=pltpu.HBM)


def on_chip(x):
    return pltpu.with_memory_space_constraint(x, pltpu.VMEM)


def in_place(x):
    return pltpu.with_memory_space_constraint(x, pltpu.HBM)


def room(mib):
    return pltpu.CompilerParams(vmem_limit_bytes=mib << 20)


def spread_kernel(m_hbm, s_hbm, out_ref, m_ref, s_ref, sem):
    rows = out_ref.shape[3]
    copies = [pltpu.make_async_copy(m_hbm, m_ref, sem.at[0]), pltpu.make_async_copy(s_hbm, s_ref, sem.at[1])]
    for copy in copies:
        copy.start()
    for copy in copies:
        copy.wait()
    for half in range(2):
        cut = slice(half * rows, (half + 1) * rows)
        for y in range(8):
            out_ref[half, y, 0:2, :] = m_ref[:, cut]
            out_ref[half, y, 2:4, :] = s_ref[:, cut]


def pick_kernel(near_ref, out_ref):
    core, yh, yl = lax.axis_index("core"), lax.axis_index("yh"), lax.axis_index("yl")
    z = 2 * lax.axis_index("zh") + lax.axis_index("zl")

    def put(piece, p, column):
        for xl in range(2):
            data = near_ref[xl, p, column : column + 2, :]
            for peer in range(4):
                out_ref[peer, piece, 2 * xl : 2 * xl + 2, :] = data

    for piece in range(8):
        y = 2 * piece + yl if piece < 4 else 2 * yh + 1 - yl
        put(piece, jnp.where(core == 0, y, piece), 0)
    put(8, z, 2)


def pack_kernel(mid_ref, out_ref):
    core, yh = lax.axis_index("core"), lax.axis_index("yh")
    for zh in range(4):
        for piece in range(5):
            n = zh * 5 + piece
            if n < 8:
                first, second = yh, n
            else:
                first, second = (n - 8 if n < 12 else 0), 8
            out_ref[n] = mid_ref[jnp.where(core == 0, zh, first), jnp.where(core == 0, piece, second)]


def tensor_kernel(near_ref, mid_ref, got_ref, keep_ref, send_ref, left, left2, mode_j, slope, prod_hi, prod_lo):
    core, yh, yl = lax.axis_index("core"), lax.axis_index("yh"), lax.axis_index("yl")
    zl = lax.axis_index("zl")

    @pl.when(core == 0)
    def _():
        for other in range(2):
            parity = 1 - zl if other else zl

            def piece_of(zh, piece):
                return got_ref[zh * 5 + piece] if other else mid_ref[zh, piece]

            block = left.at[pl.ds(pl.multiple_of(parity * 64, 64), 64)]
            for zh in range(4):
                for q in range(4):
                    row = zh * 16 + q * 4
                    block[row : row + 4, :] = piece_of(zh, q)
                modes = mode_j.at[pl.ds(pl.multiple_of(zh * 16 + parity * 8, 8), 8)]
                for y in range(2):
                    data = piece_of(zh, jnp.where(yl == y, yh, 4))
                    for xl in range(2):
                        row = xl * 4 + y * 2
                        modes[row : row + 2, :] = data[2 * xl : 2 * xl + 2, :]
        for xl in range(2):
            for y in range(8):
                row = xl * 16 + y * 2
                slope[row : row + 2, :] = near_ref[xl, y, 2:4, :]

    @pl.when(core != 0)
    def _():
        for z in range(8):
            for q in range(4):
                row = (1 - z % 2) * 64 + (z // 2) * 16 + q * 4
                left[row : row + 4, :] = mid_ref[q, z]
        for own in range(2):

            @pl.when(yl == own)
            def _():
                for y in range(2):
                    for z in range(8):
                        data = mid_ref[yh, z] if y == own else got_ref[z]
                        for xl in range(2):
                            row = z * 8 + xl * 4 + y * 2
                            mode_j[row : row + 2, :] = data[2 * xl : 2 * xl + 2, :]
                    for q in range(4):
                        data = mid_ref[q, 8] if y == own else got_ref[8 + q]
                        for xl in range(2):
                            row = xl * 16 + (2 * q + y) * 2
                            slope[row : row + 2, :] = data[2 * xl : 2 * xl + 2, :]

    whole = left[...]
    high = whole.astype(jnp.bfloat16)
    left2[0:128, :] = high
    left2[128:256, :] = (whole - high.astype(jnp.float32)).astype(jnp.bfloat16)
    lane = lax.broadcasted_iota(jnp.int32, (8, 128), 1)
    nt = (((1,), (1,)), ((), ()))

    for g in range(2):
        high_ref, low_ref = prod_hi.at[g % 2], prod_lo.at[g % 2]
        modes = mode_j[g * 32 : (g + 1) * 32, :]
        for j in range(32):
            prod = slope[...] * modes[j : j + 1, :]
            high = prod.astype(jnp.bfloat16)
            high_ref[j * 32 : (j + 1) * 32, :] = high
            low_ref[j * 32 : (j + 1) * 32, :] = (prod - high.astype(jnp.float32)).astype(jnp.bfloat16)
        one = lax.dot_general(high_ref[...], left2[...], nt, preferred_element_type=jnp.float32)
        two = lax.dot_general(low_ref[...], left2[0:128, :], nt, preferred_element_type=jnp.float32)
        both = one[:, 0:128] + (one[:, 128:256] + two)
        for t in range(8):
            tile = both[t * 128 : (t + 1) * 128, :].T
            z, xl = g * 4 + t // 2, t % 2
            for s in range(8):
                ref, xh = (keep_ref, s) if s < 4 else (send_ref, s - 4)
                top, low = tile[s * 16 : s * 16 + 8, :], tile[s * 16 + 8 : s * 16 + 16, :]
                ref[xh, z, xl, 0] = jnp.where(lane < 64, top, pltpu.roll(low, 64, 1))
                ref[xh, z, xl, 1] = jnp.where(lane < 64, pltpu.roll(top, 64, 1), low)


def finish_kernel(factor, parts_ref, out_ref):
    lane = lax.broadcasted_iota(jnp.int32, (8, 128), 1)
    for yl in range(2):
        sums = []
        for z in range(8):
            total = parts_ref[0, z, 0, yl]
            for xh in range(4):
                for xl in range(2):
                    if xh or xl:
                        total = total + parts_ref[xh, z, xl, yl]
            sums.append(total * factor)
        for h in range(2):
            for bj in range(2):
                for side in range(2):
                    wide = None
                    for p in range(4):
                        here = sums[side * 4 + p]
                        shift = (p * 32 - (h * 64 + bj * 32)) % 128
                        moved = pltpu.roll(here, shift, 1) if shift else here
                        wide = moved if wide is None else jnp.where(lane < p * 32, wide, moved)
                    for r in range(8):
                        q, xl, b = h * 2 + r // 4, (r // 2) % 2, r % 2
                        i = xl * 16 + (2 * q + yl) * 2 + b
                        out_ref[i, bj : bj + 1, side * 128 : (side + 1) * 128] = wide[r : r + 1, :]


def device(xh, core, z, xl, y):
    return (((xh * 2 + core) * 8 + z) * 2 + xl) * 8 + y


def gather_groups():
    first, second, third = [], [], []
    for xh in range(4):
        for kept in range(8):
            first.append([device(xh, 0, kept, xl, y) for xl in range(2) for y in range(8)])
            first.append([device(xh, 1, z, xl, kept) for xl in range(2) for z in range(8)])
            for xl in range(2):
                for parity in range(2):
                    second.append([device(xh, 0, parity + 2 * n, xl, kept) for n in range(4)])
                    second.append([device(xh, 1, kept, xl, parity + 2 * n) for n in range(4)])
                for n in range(8):
                    third.append((device(xh, 0, n, xl, kept), device(xh, 0, n ^ 1, xl, kept)))
                    third.append((device(xh, 1, kept, xl, n), device(xh, 1, kept, xl, n ^ 1)))
    return first, second, third


def per_device(modes_field, slopes):
    rows, own = modes_field.shape
    half = rows // 2
    f32 = jnp.float32
    factor = 1.0 / math.sqrt(rows * lax.axis_size(SPACE))
    spread = pl.pallas_call(
        spread_kernel,
        out_shape=pltpu.VMEM((2, 8, 4, half), f32),
        in_specs=[HBM, HBM],
        out_specs=VMEM,
        scratch_shapes=[
            pltpu.VMEM((own, rows), f32),
            pltpu.VMEM((own, rows), f32),
            pltpu.SemaphoreType.DMA((2,)),
        ],
        compiler_params=room(8),
    )(in_place(modes_field.T), in_place(slopes.T))
    first, second, third = gather_groups()
    near = lax.all_to_all(spread.reshape(16, 4, half), AXES, 0, 0, axis_index_groups=first, tiled=True)
    near = on_chip(near.reshape(2, 8, 4, half))
    picked = pl.pallas_call(
        pick_kernel,
        out_shape=pltpu.VMEM((4, 9, 4, half), f32),
        in_specs=[VMEM],
        out_specs=VMEM,
        compiler_params=room(8),
    )(near)
    mid = on_chip(lax.all_to_all(picked, AXES, 0, 0, axis_index_groups=second, tiled=True))
    packed = pl.pallas_call(
        pack_kernel,
        out_shape=pltpu.VMEM((20, 4, half), f32),
        in_specs=[VMEM],
        out_specs=VMEM,
        compiler_params=room(8),
    )(mid)
    got = on_chip(lax.ppermute(packed, AXES, third))
    piece = pltpu.VMEM((4, 8, 2, 2, 8, 128), f32)
    keep, send = pl.pallas_call(
        tensor_kernel,
        out_shape=(piece, piece),
        in_specs=[VMEM, VMEM, VMEM],
        out_specs=(VMEM, VMEM),
        scratch_shapes=[
            pltpu.VMEM((128, half), f32),
            pltpu.VMEM((256, half), jnp.bfloat16),
            pltpu.VMEM((64, half), f32),
            pltpu.VMEM((32, half), f32),
            pltpu.VMEM((2, 1024, half), jnp.bfloat16),
            pltpu.VMEM((2, 1024, half), jnp.bfloat16),
        ],
        compiler_params=room(24),
    )(near, mid, got)
    pair = keep + lax.ppermute(send, "core", [(0, 1), (1, 0)])
    parts = lax.all_to_all(pair.reshape(128, 8, 128), ("xh", "zh", "zl", "xl", "yl"), 0, 0, tiled=True)
    return pl.pallas_call(
        functools.partial(finish_kernel, factor),
        out_shape=jax.ShapeDtypeStruct((32, 2, 256), f32),
        in_specs=[VMEM],
        out_specs=VMEM,
        compiler_params=room(8),
    )(on_chip(parts.reshape(4, 8, 2, 2, 8, 128)))


def solution(mesh):
    fine = Mesh(mesh.devices.reshape(4, 2, 4, 2, 2, 4, 2), AXES)
    placed = P(SPACE, MODES)
    return jax.shard_map(
        per_device, mesh=fine, in_specs=(placed, placed), out_specs=P(SPACE, MODES, None), check_vma=False
    )
```

```python
import functools
import math

import jax
import jax.numpy as jnp
from jax import lax
from jax.experimental import pallas as pl
from jax.experimental.pallas import tpu as pltpu
from jax.sharding import Mesh
from jax.sharding import PartitionSpec as P

AXES = ("xh", "core", "zh", "zl", "xl", "yh", "yl")
SPACE = ("xh", "core")
MODES = ("zh", "zl", "xl", "yh", "yl")
VMEM = pl.BlockSpec(memory_space=pltpu.VMEM)
HBM = pl.BlockSpec(memory_space=pltpu.HBM)


def on_chip(x):
    return pltpu.with_memory_space_constraint(x, pltpu.VMEM)


def in_place(x):
    return pltpu.with_memory_space_constraint(x, pltpu.HBM)


def room(mib):
    return pltpu.CompilerParams(vmem_limit_bytes=mib << 20)


def spread_kernel(m_hbm, s_hbm, out_ref, m_ref, s_ref, sem):
    rows = out_ref.shape[3]
    copies = [pltpu.make_async_copy(m_hbm, m_ref, sem.at[0]), pltpu.make_async_copy(s_hbm, s_ref, sem.at[1])]
    for copy in copies:
        copy.start()
    for copy in copies:
        copy.wait()
    for half in range(2):
        cut = slice(half * rows, (half + 1) * rows)
        for y in range(8):
            out_ref[half, y, 0:2, :] = m_ref[:, cut]
            out_ref[half, y, 2:4, :] = s_ref[:, cut]


def pick_kernel(near_ref, out_ref):
    core, yh, yl = lax.axis_index("core"), lax.axis_index("yh"), lax.axis_index("yl")
    z = 2 * lax.axis_index("zh") + lax.axis_index("zl")

    def put(piece, p, column):
        for xl in range(2):
            data = near_ref[xl, p, column : column + 2, :]
            for peer in range(4):
                out_ref[peer, piece, 2 * xl : 2 * xl + 2, :] = data

    for piece in range(8):
        y = 2 * piece + yl if piece < 4 else 2 * yh + 1 - yl
        put(piece, jnp.where(core == 0, y, piece), 0)
    put(8, z, 2)


def pack_kernel(mid_ref, up_ref, down_ref):
    core, yh, yl = lax.axis_index("core"), lax.axis_index("yh"), lax.axis_index("yl")
    for half, out_ref in ((0, up_ref), (1, down_ref)):
        theirs = lax.rem(yh + yl + (4 if half == 0 else 3), 4)
        for n in range(10):
            if n < 4:
                first, second = theirs, 4 * half + n
            else:
                first, second = 2 * half + n % 2, 8
            zh, piece = 2 * half + n // 5, n % 5
            out_ref[n] = mid_ref[jnp.where(core == 0, zh, first), jnp.where(core == 0, piece, second)]


def tensor_kernel(near_ref, mid_ref, below_ref, above_ref, keep_ref, send_ref, left, left2, mode_j, slope, prod_hi, prod_lo):
    core, yh, yl = lax.axis_index("core"), lax.axis_index("yh"), lax.axis_index("yl")
    zl = lax.axis_index("zl")

    @pl.when(core == 0)
    def _():
        for other in range(2):
            parity = 1 - zl if other else zl

            def piece_of(zh, piece):
                if not other:
                    return mid_ref[zh, piece]
                return (below_ref if zh < 2 else above_ref)[zh % 2 * 5 + piece]

            block = left.at[pl.ds(pl.multiple_of(parity * 64, 64), 64)]
            for zh in range(4):
                for q in range(4):
                    row = zh * 16 + q * 4
                    block[row : row + 4, :] = piece_of(zh, q)
                modes = mode_j.at[pl.ds(pl.multiple_of(zh * 16 + parity * 8, 8), 8)]
                for y in range(2):
                    data = piece_of(zh, jnp.where(yl == y, yh, 4))
                    for xl in range(2):
                        row = xl * 4 + y * 2
                        modes[row : row + 2, :] = data[2 * xl : 2 * xl + 2, :]
        for xl in range(2):
            for y in range(8):
                row = xl * 16 + y * 2
                slope[row : row + 2, :] = near_ref[xl, y, 2:4, :]

    @pl.when(core != 0)
    def _():
        for z in range(8):
            for q in range(4):
                row = (1 - z % 2) * 64 + (z // 2) * 16 + q * 4
                left[row : row + 4, :] = mid_ref[q, z]
        for own in range(2):

            @pl.when(yl == own)
            def _():
                for y in range(2):
                    for z in range(8):
                        data = mid_ref[yh, z] if y == own else (below_ref if z < 4 else above_ref)[z % 4]
                        for xl in range(2):
                            row = z * 8 + xl * 4 + y * 2
                            mode_j[row : row + 2, :] = data[2 * xl : 2 * xl + 2, :]
                    for q in range(4):
                        data = mid_ref[q, 8] if y == own else (below_ref if q < 2 else above_ref)[4 + q % 2]
                        for xl in range(2):
                            row = xl * 16 + (2 * q + y) * 2
                            slope[row : row + 2, :] = data[2 * xl : 2 * xl + 2, :]

    whole = left[...]
    high = whole.astype(jnp.bfloat16)
    left2[0:128, :] = high
    left2[128:256, :] = (whole - high.astype(jnp.float32)).astype(jnp.bfloat16)
    lane = lax.broadcasted_iota(jnp.int32, (8, 128), 1)
    nt = (((1,), (1,)), ((), ()))

    for g in range(2):
        high_ref, low_ref = prod_hi.at[g % 2], prod_lo.at[g % 2]
        modes = mode_j[g * 32 : (g + 1) * 32, :]
        for j in range(32):
            prod = slope[...] * modes[j : j + 1, :]
            high = prod.astype(jnp.bfloat16)
            high_ref[j * 32 : (j + 1) * 32, :] = high
            low_ref[j * 32 : (j + 1) * 32, :] = (prod - high.astype(jnp.float32)).astype(jnp.bfloat16)
        one = lax.dot_general(high_ref[...], left2[...], nt, preferred_element_type=jnp.float32)
        two = lax.dot_general(low_ref[...], left2[0:128, :], nt, preferred_element_type=jnp.float32)
        both = one[:, 0:128] + (one[:, 128:256] + two)
        for t in range(8):
            tile = both[t * 128 : (t + 1) * 128, :].T
            z, xl = g * 4 + t // 2, t % 2
            for s in range(8):
                ref, xh = (keep_ref, s) if s < 4 else (send_ref, s - 4)
                top, low = tile[s * 16 : s * 16 + 8, :], tile[s * 16 + 8 : s * 16 + 16, :]
                ref[xh, z, xl, 0] = jnp.where(lane < 64, top, pltpu.roll(low, 64, 1))
                ref[xh, z, xl, 1] = jnp.where(lane < 64, pltpu.roll(top, 64, 1), low)


def finish_kernel(factor, parts_ref, out_ref):
    lane = lax.broadcasted_iota(jnp.int32, (8, 128), 1)
    for yl in range(2):
        sums = []
        for z in range(8):
            total = parts_ref[0, z, 0, yl]
            for xh in range(4):
                for xl in range(2):
                    if xh or xl:
                        total = total + parts_ref[xh, z, xl, yl]
            sums.append(total * factor)
        for h in range(2):
            for bj in range(2):
                for side in range(2):
                    wide = None
                    for p in range(4):
                        here = sums[side * 4 + p]
                        shift = (p * 32 - (h * 64 + bj * 32)) % 128
                        moved = pltpu.roll(here, shift, 1) if shift else here
                        wide = moved if wide is None else jnp.where(lane < p * 32, wide, moved)
                    for r in range(8):
                        q, xl, b = h * 2 + r // 4, (r // 2) % 2, r % 2
                        i = xl * 16 + (2 * q + yl) * 2 + b
                        out_ref[i, bj : bj + 1, side * 128 : (side + 1) * 128] = wide[r : r + 1, :]


def device(xh, core, z, xl, y):
    return (((xh * 2 + core) * 8 + z) * 2 + xl) * 8 + y


def gather_groups():
    first, second, third = [], [], []
    for xh in range(4):
        for kept in range(8):
            first.append([device(xh, 0, kept, xl, y) for xl in range(2) for y in range(8)])
            first.append([device(xh, 1, z, xl, kept) for xl in range(2) for z in range(8)])
            for xl in range(2):
                for parity in range(2):
                    second.append([device(xh, 0, parity + 2 * n, xl, kept) for n in range(4)])
                    second.append([device(xh, 1, kept, xl, parity + 2 * n) for n in range(4)])
                for n in range(8):
                    third.append((device(xh, 0, n, xl, kept), device(xh, 0, (n + 1) % 8, xl, kept)))
                    third.append((device(xh, 1, kept, xl, n), device(xh, 1, kept, xl, (n + 1) % 8)))
    return first, second, third


def per_device(modes_field, slopes):
    rows, own = modes_field.shape
    half = rows // 2
    f32 = jnp.float32
    factor = 1.0 / math.sqrt(rows * lax.axis_size(SPACE))
    spread = pl.pallas_call(
        spread_kernel,
        out_shape=pltpu.VMEM((2, 8, 4, half), f32),
        in_specs=[HBM, HBM],
        out_specs=VMEM,
        scratch_shapes=[
            pltpu.VMEM((own, rows), f32),
            pltpu.VMEM((own, rows), f32),
            pltpu.SemaphoreType.DMA((2,)),
        ],
        compiler_params=room(8),
    )(in_place(modes_field.T), in_place(slopes.T))
    first, second, third = gather_groups()
    near = lax.all_to_all(spread.reshape(16, 4, half), AXES, 0, 0, axis_index_groups=first, tiled=True)
    near = on_chip(near.reshape(2, 8, 4, half))
    picked = pl.pallas_call(
        pick_kernel,
        out_shape=pltpu.VMEM((4, 9, 4, half), f32),
        in_specs=[VMEM],
        out_specs=VMEM,
        compiler_params=room(8),
    )(near)
    mid = on_chip(lax.all_to_all(picked, AXES, 0, 0, axis_index_groups=second, tiled=True))
    ten = pltpu.VMEM((10, 4, half), f32)
    up, down = pl.pallas_call(
        pack_kernel,
        out_shape=(ten, ten),
        in_specs=[VMEM],
        out_specs=(VMEM, VMEM),
        compiler_params=room(8),
    )(mid)
    below = on_chip(lax.ppermute(up, AXES, third))
    above = on_chip(lax.ppermute(down, AXES, [(b, a) for a, b in third]))
    piece = pltpu.VMEM((4, 8, 2, 2, 8, 128), f32)
    keep, send = pl.pallas_call(
        tensor_kernel,
        out_shape=(piece, piece),
        in_specs=[VMEM] * 4,
        out_specs=(VMEM, VMEM),
        scratch_shapes=[
            pltpu.VMEM((128, half), f32),
            pltpu.VMEM((256, half), jnp.bfloat16),
            pltpu.VMEM((64, half), f32),
            pltpu.VMEM((32, half), f32),
            pltpu.VMEM((2, 1024, half), jnp.bfloat16),
            pltpu.VMEM((2, 1024, half), jnp.bfloat16),
        ],
        compiler_params=room(24),
    )(near, mid, below, above)
    pair = keep + lax.ppermute(send, "core", [(0, 1), (1, 0)])
    parts = lax.all_to_all(pair.reshape(128, 8, 128), ("xh", "zh", "zl", "xl", "yl"), 0, 0, tiled=True)
    return pl.pallas_call(
        functools.partial(finish_kernel, factor),
        out_shape=jax.ShapeDtypeStruct((32, 2, 256), f32),
        in_specs=[VMEM],
        out_specs=VMEM,
        compiler_params=room(8),
    )(on_chip(parts.reshape(4, 8, 2, 2, 8, 128)))


def solution(mesh):
    fine = Mesh(mesh.devices.reshape(4, 2, 4, 2, 2, 4, 2), AXES)
    placed = P(SPACE, MODES)
    return jax.shard_map(
        per_device, mesh=fine, in_specs=(placed, placed), out_specs=P(SPACE, MODES, None), check_vma=False
    )
```

```python
import functools
import math

import jax
import jax.numpy as jnp
from jax import lax
from jax.experimental import pallas as pl
from jax.experimental.pallas import tpu as pltpu
from jax.sharding import Mesh
from jax.sharding import PartitionSpec as P

AXES = ("xh", "core", "z", "xl", "yh", "yl")
SPACE = ("xh", "core")
MODES = ("z", "xl", "yh", "yl")
VMEM = pl.BlockSpec(memory_space=pltpu.VMEM)
HBM = pl.BlockSpec(memory_space=pltpu.HBM)


def on_chip(x):
    return pltpu.with_memory_space_constraint(x, pltpu.VMEM)


def in_place(x):
    return pltpu.with_memory_space_constraint(x, pltpu.HBM)


def room(mib):
    return pltpu.CompilerParams(vmem_limit_bytes=mib << 20)


def spread_kernel(m_hbm, s_hbm, out_ref, m_ref, s_ref, sem):
    rows = out_ref.shape[3]
    copies = [pltpu.make_async_copy(m_hbm, m_ref, sem.at[0]), pltpu.make_async_copy(s_hbm, s_ref, sem.at[1])]
    for copy in copies:
        copy.start()
    for copy in copies:
        copy.wait()
    for half in range(2):
        cut = slice(half * rows, (half + 1) * rows)
        for y in range(8):
            out_ref[half, y, 0:2, :] = m_ref[:, cut]
            out_ref[half, y, 2:4, :] = s_ref[:, cut]


def pick_kernel(near_ref, out_ref):
    core, yh, yl = lax.axis_index("core"), lax.axis_index("yh"), lax.axis_index("yl")
    z = lax.axis_index("z")

    def put(piece, p, column):
        for xl in range(2):
            data = near_ref[xl, p, column : column + 2, :]
            for peer in range(8):
                out_ref[peer, piece, 2 * xl : 2 * xl + 2, :] = data

    for piece in range(8):
        y = 2 * piece + yl if piece < 4 else 2 * yh + 1 - yl
        put(piece, jnp.where(core == 0, y, piece), 0)
    put(8, z, 2)


def tensor_kernel(near_ref, far_ref, keep_ref, send_ref, left, left2, mode_j, slope, prod_hi, prod_lo):
    core, yh, yl = lax.axis_index("core"), lax.axis_index("yh"), lax.axis_index("yl")

    def far(z, y, piece):
        return jnp.where(core == 0, z, y), jnp.where(core == 0, piece, z)

    for rel in range(2):
        for xh in range(4):
            z = 2 * xh + (core if rel == 0 else 1 - core)
            for q in range(4):
                row = rel * 64 + xh * 16 + q * 4
                peer, piece = far(z, 2 * q + yl, q)
                left[row : row + 4, :] = far_ref[peer, piece]
    for y in range(2):
        for z in range(8):
            peer, piece = far(z, 2 * yh + y, jnp.where(yl == y, yh, 4))
            for xl in range(2):
                row = z * 8 + xl * 4 + y * 2
                mode_j[row : row + 2, :] = far_ref[peer, piece, 2 * xl : 2 * xl + 2, :]

    @pl.when(core == 0)
    def _():
        for xl in range(2):
            for y in range(8):
                row = xl * 16 + y * 2
                slope[row : row + 2, :] = near_ref[xl, y, 2:4, :]

    @pl.when(core != 0)
    def _():
        for xl in range(2):
            for y in range(8):
                row = xl * 16 + y * 2
                slope[row : row + 2, :] = far_ref[y, 8, 2 * xl : 2 * xl + 2, :]

    whole = left[...]
    high = whole.astype(jnp.bfloat16)
    left2[0:128, :] = high
    left2[128:256, :] = (whole - high.astype(jnp.float32)).astype(jnp.bfloat16)
    lane = lax.broadcasted_iota(jnp.int32, (8, 128), 1)
    nt = (((1,), (1,)), ((), ()))

    for g in range(2):
        high_ref, low_ref = prod_hi.at[g % 2], prod_lo.at[g % 2]
        modes = mode_j[g * 32 : (g + 1) * 32, :]
        for j in range(32):
            prod = slope[...] * modes[j : j + 1, :]
            high = prod.astype(jnp.bfloat16)
            high_ref[j * 32 : (j + 1) * 32, :] = high
            low_ref[j * 32 : (j + 1) * 32, :] = (prod - high.astype(jnp.float32)).astype(jnp.bfloat16)
        one = lax.dot_general(high_ref[...], left2[...], nt, preferred_element_type=jnp.float32)
        two = lax.dot_general(low_ref[...], left2[0:128, :], nt, preferred_element_type=jnp.float32)
        both = one[:, 0:128] + (one[:, 128:256] + two)
        for t in range(8):
            tile = both[t * 128 : (t + 1) * 128, :].T
            z, xl = g * 4 + t // 2, t % 2
            for s in range(8):
                ref, xh = (keep_ref, s) if s < 4 else (send_ref, s - 4)
                top, low = tile[s * 16 : s * 16 + 8, :], tile[s * 16 + 8 : s * 16 + 16, :]
                ref[0, xl, z, xh] = jnp.where(lane < 64, top, pltpu.roll(low, 64, 1))
                ref[1, xl, z, xh] = jnp.where(lane < 64, pltpu.roll(top, 64, 1), low)


def finish_kernel(factor, parts_ref, out_ref):
    lane = lax.broadcasted_iota(jnp.int32, (8, 128), 1)
    for yl in range(2):
        sums = []
        for z in range(8):
            total = parts_ref[yl, 0, z, 0]
            for xh in range(4):
                for xl in range(2):
                    if xh or xl:
                        total = total + parts_ref[yl, xl, z, xh]
            sums.append(total * factor)
        for h in range(2):
            for bj in range(2):
                for side in range(2):
                    wide = None
                    for p in range(4):
                        here = sums[side * 4 + p]
                        shift = (p * 32 - (h * 64 + bj * 32)) % 128
                        moved = pltpu.roll(here, shift, 1) if shift else here
                        wide = moved if wide is None else jnp.where(lane < p * 32, wide, moved)
                    for r in range(8):
                        q, xl, b = h * 2 + r // 4, (r // 2) % 2, r % 2
                        i = xl * 16 + (2 * q + yl) * 2 + b
                        out_ref[i, bj : bj + 1, side * 128 : (side + 1) * 128] = wide[r : r + 1, :]


def gather_groups():
    first, second = [], []
    for xh in range(4):
        for core in range(2):
            for kept in range(8):
                for xl in range(2):
                    line = []
                    for moved in range(8):
                        z, y = (kept, moved) if core == 0 else (moved, kept)
                        line.append((((xh * 2 + core) * 8 + z) * 2 + xl) * 8 + y)
                    first.append(line)
    first = [first[n] + first[n + 1] for n in range(0, len(first), 2)]
    for xh in range(4):
        for core in range(2):
            for xl in range(2):
                for kept in range(8):
                    line = []
                    for moved in range(8):
                        z, y = (moved, kept) if core == 0 else (kept, moved)
                        line.append((((xh * 2 + core) * 8 + z) * 2 + xl) * 8 + y)
                    second.append(line)
    return first, second


def owner_groups():
    return [
        [
            (((xh * 2 + core) * 8 + z) * 2 + xl) * 8 + yh * 2 + yl
            for yl in range(2)
            for xl in range(2)
            for z in range(8)
            for xh in range(4)
        ]
        for core in range(2)
        for yh in range(4)
    ]


def per_device(modes_field, slopes):
    rows, own = modes_field.shape
    half = rows // 2
    f32 = jnp.float32
    factor = 1.0 / math.sqrt(rows * lax.axis_size(SPACE))
    spread = pl.pallas_call(
        spread_kernel,
        out_shape=pltpu.VMEM((2, 8, 4, half), f32),
        in_specs=[HBM, HBM],
        out_specs=VMEM,
        scratch_shapes=[
            pltpu.VMEM((own, rows), f32),
            pltpu.VMEM((own, rows), f32),
            pltpu.SemaphoreType.DMA((2,)),
        ],
        compiler_params=room(8),
    )(in_place(modes_field.T), in_place(slopes.T))
    first, second = gather_groups()
    near = lax.all_to_all(spread.reshape(16, 4, half), AXES, 0, 0, axis_index_groups=first, tiled=True)
    near = on_chip(near.reshape(2, 8, 4, half))
    picked = pl.pallas_call(
        pick_kernel,
        out_shape=pltpu.VMEM((8, 9, 4, half), f32),
        in_specs=[VMEM],
        out_specs=VMEM,
        compiler_params=room(8),
    )(near)
    far = on_chip(lax.all_to_all(picked, AXES, 0, 0, axis_index_groups=second, tiled=True))
    piece = pltpu.VMEM((2, 2, 8, 4, 8, 128), f32)
    keep, send = pl.pallas_call(
        tensor_kernel,
        out_shape=(piece, piece),
        in_specs=[VMEM, VMEM],
        out_specs=(VMEM, VMEM),
        scratch_shapes=[
            pltpu.VMEM((128, half), f32),
            pltpu.VMEM((256, half), jnp.bfloat16),
            pltpu.VMEM((64, half), f32),
            pltpu.VMEM((32, half), f32),
            pltpu.VMEM((2, 1024, half), jnp.bfloat16),
            pltpu.VMEM((2, 1024, half), jnp.bfloat16),
        ],
        compiler_params=room(24),
    )(near, far)
    pair = keep + lax.ppermute(send, "core", [(0, 1), (1, 0)])
    parts = lax.all_to_all(pair.reshape(128, 8, 128), AXES, 0, 0, axis_index_groups=owner_groups(), tiled=True)
    return pl.pallas_call(
        functools.partial(finish_kernel, factor),
        out_shape=jax.ShapeDtypeStruct((32, 2, 256), f32),
        in_specs=[VMEM],
        out_specs=VMEM,
        compiler_params=room(8),
    )(on_chip(parts.reshape(2, 2, 8, 4, 8, 128)))


def solution(mesh):
    fine = Mesh(mesh.devices.reshape(4, 2, 8, 2, 4, 2), AXES)
    placed = P(SPACE, MODES)
    return jax.shard_map(
        per_device, mesh=fine, in_specs=(placed, placed), out_specs=P(SPACE, MODES, None), check_vma=False
    )
```

```python
import functools
import math

import jax
import jax.numpy as jnp
from jax import lax
from jax.experimental import pallas as pl
from jax.experimental.pallas import tpu as pltpu
from jax.sharding import Mesh
from jax.sharding import PartitionSpec as P

AXES = ("xh", "core", "zh", "zl", "xl", "yh", "yl")
SPACE = ("xh", "core")
MODES = ("zh", "zl", "xl", "yh", "yl")
VMEM = pl.BlockSpec(memory_space=pltpu.VMEM)
HBM = pl.BlockSpec(memory_space=pltpu.HBM)


def on_chip(x):
    return pltpu.with_memory_space_constraint(x, pltpu.VMEM)


def in_place(x):
    return pltpu.with_memory_space_constraint(x, pltpu.HBM)


def room(mib):
    return pltpu.CompilerParams(vmem_limit_bytes=mib << 20)


def spread_kernel(m_hbm, s_hbm, out_ref, m_ref, s_ref, sem):
    rows = out_ref.shape[3]
    copies = [pltpu.make_async_copy(m_hbm, m_ref, sem.at[0]), pltpu.make_async_copy(s_hbm, s_ref, sem.at[1])]
    for copy in copies:
        copy.start()
    for copy in copies:
        copy.wait()
    for half in range(2):
        cut = slice(half * rows, (half + 1) * rows)
        for y in range(8):
            out_ref[half, y, 0:2, :] = m_ref[:, cut]
            out_ref[half, y, 2:4, :] = s_ref[:, cut]


def pick_kernel(near_ref, out_ref):
    core, yh, yl = lax.axis_index("core"), lax.axis_index("yh"), lax.axis_index("yl")
    z = 2 * lax.axis_index("zh") + lax.axis_index("zl")

    def put(piece, p, column):
        for xl in range(2):
            data = near_ref[xl, p, column : column + 2, :]
            for peer in range(4):
                out_ref[peer, piece, 2 * xl : 2 * xl + 2, :] = data

    for piece in range(8):
        y = 2 * piece + yl if piece < 4 else 2 * yh + 1 - yl
        put(piece, jnp.where(core == 0, y, piece), 0)
    put(8, z, 2)


def pack_kernel(mid_ref, out_ref):
    core, yh = lax.axis_index("core"), lax.axis_index("yh")
    other = 1 - jnp.where(core == 0, lax.axis_index("zl"), lax.axis_index("yl"))
    for zh in range(4):
        for piece in range(5):
            n = zh * 5 + piece
            if n < 8:
                first, second = yh, n
            else:
                first, second = (n - 8 if n < 12 else 0), 8
            out_ref[other, n] = mid_ref[jnp.where(core == 0, zh, first), jnp.where(core == 0, piece, second)]


def tensor_kernel(near_ref, mid_ref, got_ref, keep_ref, send_ref, left, left2, mode_j, slope, prod_hi, prod_lo):
    core, yh, yl = lax.axis_index("core"), lax.axis_index("yh"), lax.axis_index("yl")
    zl = lax.axis_index("zl")

    @pl.when(core == 0)
    def _():
        for other in range(2):
            parity = 1 - zl if other else zl

            def piece_of(zh, piece):
                return got_ref[1 - zl, zh * 5 + piece] if other else mid_ref[zh, piece]

            block = left.at[pl.ds(pl.multiple_of(parity * 64, 64), 64)]
            for zh in range(4):
                for q in range(4):
                    row = zh * 16 + q * 4
                    block[row : row + 4, :] = piece_of(zh, q)
                modes = mode_j.at[pl.ds(pl.multiple_of(zh * 16 + parity * 8, 8), 8)]
                for y in range(2):
                    data = piece_of(zh, jnp.where(yl == y, yh, 4))
                    for xl in range(2):
                        row = xl * 4 + y * 2
                        modes[row : row + 2, :] = data[2 * xl : 2 * xl + 2, :]
        for xl in range(2):
            for y in range(8):
                row = xl * 16 + y * 2
                slope[row : row + 2, :] = near_ref[xl, y, 2:4, :]

    @pl.when(core != 0)
    def _():
        for z in range(8):
            for q in range(4):
                row = (1 - z % 2) * 64 + (z // 2) * 16 + q * 4
                left[row : row + 4, :] = mid_ref[q, z]
        for own in range(2):

            @pl.when(yl == own)
            def _():
                for y in range(2):
                    for z in range(8):
                        data = mid_ref[yh, z] if y == own else got_ref[1 - own, z]
                        for xl in range(2):
                            row = z * 8 + xl * 4 + y * 2
                            mode_j[row : row + 2, :] = data[2 * xl : 2 * xl + 2, :]
                    for q in range(4):
                        data = mid_ref[q, 8] if y == own else got_ref[1 - own, 8 + q]
                        for xl in range(2):
                            row = xl * 16 + (2 * q + y) * 2
                            slope[row : row + 2, :] = data[2 * xl : 2 * xl + 2, :]

    whole = left[...]
    high = whole.astype(jnp.bfloat16)
    left2[0:128, :] = high
    left2[128:256, :] = (whole - high.astype(jnp.float32)).astype(jnp.bfloat16)
    lane = lax.broadcasted_iota(jnp.int32, (8, 128), 1)
    nt = (((1,), (1,)), ((), ()))

    for g in range(2):
        high_ref, low_ref = prod_hi.at[g % 2], prod_lo.at[g % 2]
        modes = mode_j[g * 32 : (g + 1) * 32, :]
        for j in range(32):
            prod = slope[...] * modes[j : j + 1, :]
            high = prod.astype(jnp.bfloat16)
            high_ref[j * 32 : (j + 1) * 32, :] = high
            low_ref[j * 32 : (j + 1) * 32, :] = (prod - high.astype(jnp.float32)).astype(jnp.bfloat16)
        one = lax.dot_general(high_ref[...], left2[...], nt, preferred_element_type=jnp.float32)
        two = lax.dot_general(low_ref[...], left2[0:128, :], nt, preferred_element_type=jnp.float32)
        both = one[:, 0:128] + (one[:, 128:256] + two)
        for t in range(8):
            tile = both[t * 128 : (t + 1) * 128, :].T
            z, xl = g * 4 + t // 2, t % 2
            for s in range(8):
                ref, xh = (keep_ref, s) if s < 4 else (send_ref, s - 4)
                top, low = tile[s * 16 : s * 16 + 8, :], tile[s * 16 + 8 : s * 16 + 16, :]
                ref[xh, z, xl, 0] = jnp.where(lane < 64, top, pltpu.roll(low, 64, 1))
                ref[xh, z, xl, 1] = jnp.where(lane < 64, pltpu.roll(top, 64, 1), low)


def finish_kernel(factor, parts_ref, out_ref):
    lane = lax.broadcasted_iota(jnp.int32, (8, 128), 1)
    for yl in range(2):
        sums = []
        for z in range(8):
            total = parts_ref[0, z, 0, yl]
            for xh in range(4):
                for xl in range(2):
                    if xh or xl:
                        total = total + parts_ref[xh, z, xl, yl]
            sums.append(total * factor)
        for h in range(2):
            for bj in range(2):
                for side in range(2):
                    wide = None
                    for p in range(4):
                        here = sums[side * 4 + p]
                        shift = (p * 32 - (h * 64 + bj * 32)) % 128
                        moved = pltpu.roll(here, shift, 1) if shift else here
                        wide = moved if wide is None else jnp.where(lane < p * 32, wide, moved)
                    for r in range(8):
                        q, xl, b = h * 2 + r // 4, (r // 2) % 2, r % 2
                        i = xl * 16 + (2 * q + yl) * 2 + b
                        out_ref[i, bj : bj + 1, side * 128 : (side + 1) * 128] = wide[r : r + 1, :]


def device(xh, core, z, xl, y):
    return (((xh * 2 + core) * 8 + z) * 2 + xl) * 8 + y


def gather_groups():
    first, second, third = [], [], []
    for xh in range(4):
        for kept in range(8):
            first.append([device(xh, 0, kept, xl, y) for xl in range(2) for y in range(8)])
            first.append([device(xh, 1, z, xl, kept) for xl in range(2) for z in range(8)])
            for xl in range(2):
                for parity in range(2):
                    second.append([device(xh, 0, parity + 2 * n, xl, kept) for n in range(4)])
                    second.append([device(xh, 1, kept, xl, parity + 2 * n) for n in range(4)])
                for n in range(0, 8, 2):
                    third.append([device(xh, 0, n, xl, kept), device(xh, 0, n + 1, xl, kept)])
                    third.append([device(xh, 1, kept, xl, n), device(xh, 1, kept, xl, n + 1)])
    return first, second, third


def per_device(modes_field, slopes):
    rows, own = modes_field.shape
    half = rows // 2
    f32 = jnp.float32
    factor = 1.0 / math.sqrt(rows * lax.axis_size(SPACE))
    spread = pl.pallas_call(
        spread_kernel,
        out_shape=pltpu.VMEM((2, 8, 4, half), f32),
        in_specs=[HBM, HBM],
        out_specs=VMEM,
        scratch_shapes=[
            pltpu.VMEM((own, rows), f32),
            pltpu.VMEM((own, rows), f32),
            pltpu.SemaphoreType.DMA((2,)),
        ],
        compiler_params=room(8),
    )(in_place(modes_field.T), in_place(slopes.T))
    first, second, third = gather_groups()
    near = lax.all_to_all(spread.reshape(16, 4, half), AXES, 0, 0, axis_index_groups=first, tiled=True)
    near = on_chip(near.reshape(2, 8, 4, half))
    picked = pl.pallas_call(
        pick_kernel,
        out_shape=pltpu.VMEM((4, 9, 4, half), f32),
        in_specs=[VMEM],
        out_specs=VMEM,
        compiler_params=room(8),
    )(near)
    mid = on_chip(lax.all_to_all(picked, AXES, 0, 0, axis_index_groups=second, tiled=True))
    packed = pl.pallas_call(
        pack_kernel,
        out_shape=pltpu.VMEM((2, 20, 4, half), f32),
        in_specs=[VMEM],
        out_specs=VMEM,
        compiler_params=room(8),
    )(mid)
    got = on_chip(lax.all_to_all(packed, AXES, 0, 0, axis_index_groups=third, tiled=True))
    piece = pltpu.VMEM((4, 8, 2, 2, 8, 128), f32)
    keep, send = pl.pallas_call(
        tensor_kernel,
        out_shape=(piece, piece),
        in_specs=[VMEM, VMEM, VMEM],
        out_specs=(VMEM, VMEM),
        scratch_shapes=[
            pltpu.VMEM((128, half), f32),
            pltpu.VMEM((256, half), jnp.bfloat16),
            pltpu.VMEM((64, half), f32),
            pltpu.VMEM((32, half), f32),
            pltpu.VMEM((2, 1024, half), jnp.bfloat16),
            pltpu.VMEM((2, 1024, half), jnp.bfloat16),
        ],
        compiler_params=room(24),
    )(near, mid, got)
    pair = keep + lax.ppermute(send, "core", [(0, 1), (1, 0)])
    parts = lax.all_to_all(pair.reshape(128, 8, 128), ("xh", "zh", "zl", "xl", "yl"), 0, 0, tiled=True)
    return pl.pallas_call(
        functools.partial(finish_kernel, factor),
        out_shape=jax.ShapeDtypeStruct((32, 2, 256), f32),
        in_specs=[VMEM],
        out_specs=VMEM,
        compiler_params=room(8),
    )(on_chip(parts.reshape(4, 8, 2, 2, 8, 128)))


def solution(mesh):
    fine = Mesh(mesh.devices.reshape(4, 2, 4, 2, 2, 4, 2), AXES)
    placed = P(SPACE, MODES)
    return jax.shard_map(
        per_device, mesh=fine, in_specs=(placed, placed), out_specs=P(SPACE, MODES, None), check_vma=False
    )
```
